32 devices in a mesh: tm: 4 (over x, core), chan: 8 (over z, y).
Axes of the slice: x: 2, y: 2, z: 4, core: 2. Of those that a mesh axis runs over, the one named last changes fastest.
Arguments:
- samples: bfloat16 [384, 128], P('chan', 'tm'), may hold values from -6 to 6
- dead_channels: int32 [12], replicated, may hold values from 0 to 383
- first_kernel: bfloat16 [8, 32], replicated, may hold values from -3 to 3
- dilated_one: bfloat16 [3, 32, 64], replicated, may hold values from -0.875 to 0.875
- dilated_two: bfloat16 [3, 64, 128], replicated, may hold values from -0.625 to 0.625
- dilated_three: bfloat16 [3, 128, 256], replicated, may hold values from -0.4375 to 0.4375
- dilated_four: bfloat16 [3, 256, 256], replicated, may hold values from -0.3125 to 0.3125
- embed_weight: bfloat16 [256, 512], replicated, may hold values from -0.375 to 0.375
- gain_one: float32 [512], replicated, may hold values from 0.1 to 1.9
- project_in: bfloat16 [512, 1536], replicated, may hold values from -1 to 1
- project_out: bfloat16 [512, 512], replicated, may hold values from -0.25 to 0.25
- gain_two: float32 [512], replicated, may hold values from 0.1 to 1.9
- up_weight: bfloat16 [512, 2048], replicated, may hold values from -0.25 to 0.25
- down_weight: bfloat16 [2048, 512], replicated, may hold values from -0.125 to 0.125
Outputs:
- encoded: bfloat16 [32, 384, 512], P('tm', 'chan')
The draws below stay inside these ranges and needn't reach their ends.
Inputs may be any that keep to these rules, and one draw needn't show every extreme that they name: `dead_channels`: channel numbers; a number may repeat.
All inputs are finite; a program needn't handle non-finite values.
Results may differ from the reference program's by a relative error of at most 0.015.
Values may be sent and summed in bfloat16 or wider, within the bound.
A program may use at most 64 MiB of HBM per device.

```python
import jax
import jax.numpy as jnp
from jax import lax

D = 512
HEADS = 8
FF = 2048
C1 = 32
C2 = 64
C3 = 128
C4 = 256
KERNEL = 8
STRIDE = 4
NC = 384
F = 32
NS = 128
NDEAD = 12


def draw_project_in(key, part):
    first, second, third = jax.random.split(jax.random.fold_in(key, 11), 3)
    scaling = D ** (-0.5)
    queries = jax.random.normal(first, (D, D), jnp.float32) * scaling
    keys_part = jax.random.normal(second, (D, D), jnp.float32) * scaling
    values_part = jax.random.normal(third, (D, D), jnp.float32) * scaling
    joined = jnp.concatenate([queries, keys_part, values_part], axis=1)
    return jnp.clip(joined, -1.0, 1.0).astype(jnp.bfloat16)


def plant(result, stream_key, low, high):
    index_at = [jax.random.randint(jax.random.fold_in(stream_key, axis), (), 0, length) for axis, length in enumerate(result.shape)]
    widest = result.shape.index(max(result.shape))
    neighbour = index_at[:widest] + [(index_at[widest] + 1) % result.shape[widest]] + index_at[widest + 1:]
    return result.at[tuple(index_at)].set(low).at[tuple(neighbour)].set(high)


def steps_of(stream_key, shape, cuts, smallest, top_value):
    level, own = 1.0, jax.random.fold_in(stream_key, 6)
    for dim, blocks in cuts:
        draws = jnp.exp(jax.random.uniform(jax.random.fold_in(own, dim), (blocks,), jnp.float32, smallest / len(cuts), top_value / len(cuts)))
        level = level * jnp.repeat(draws, shape[dim] // blocks).reshape([-1 if axis == dim else 1 for axis in range(len(shape))])
    return level


def noise(stream_key, dims, deviation, limit, cuts=(), kind=jnp.bfloat16):
    entries = jax.random.normal(stream_key, dims, jnp.float32) * deviation
    if len(cuts) > 0:
        entries = steps_of(stream_key, dims, cuts, -0.22, 0.18) * entries
    return jnp.clip(entries, min=-limit, max=limit).astype(kind)


def setup_inputs(seed: int = 0) -> dict:
    streams_of = jax.random.split(jax.random.key(seed), 15)
    return {
        "samples": noise(streams_of[0], (NC, NS), 1.0, 6.0, ((0, 8), (1, 4))),
        "dead_channels": plant(jax.random.randint(streams_of[1], (NDEAD,), 0, NC), jax.random.fold_in(streams_of[1], 1), 0, NC - 1).astype(jnp.int32),
        "first_kernel": noise(streams_of[2], (KERNEL, C1), (KERNEL // 2) ** -0.5, 3.0),
        "dilated_one": noise(streams_of[3], (3, C1, C2), (3 * C1 // 2) ** -0.5, 0.875),
        "dilated_two": noise(streams_of[4], (3, C2, C3), (3 * C2 // 2) ** -0.5, 0.625),
        "dilated_three": noise(streams_of[5], (3, C3, C4), (3 * C3 // 2) ** -0.5, 0.4375),
        "dilated_four": noise(streams_of[6], (3, C4, C4), (3 * C4 // 2) ** -0.5, 0.3125),
        "embed_weight": noise(streams_of[7], (C4, D), C4 ** -0.5, 0.375),
        "gain_one": jnp.clip(1.0 + 0.18 * jax.random.normal(streams_of[8], (D,), jnp.float32), 0.1, 1.9),
        "project_in": draw_project_in(jax.random.fold_in(streams_of[14], 71), 0),
        "project_out": noise(streams_of[10], (D, D), D ** -0.5, 0.25),
        "gain_two": jnp.clip(1.0 + 0.18 * jax.random.normal(streams_of[11], (D,), jnp.float32), 0.1, 1.9),
        "up_weight": noise(streams_of[12], (D, FF), D ** -0.5, 0.25),
        "down_weight": noise(streams_of[13], (FF, D), FF ** -0.5, 0.125),
    }


EPSILON = 1e-05
DILATIONS = (1, 2, 4, 8)

def normalize(tokens, gain):
    floats = tokens.astype(jnp.float32)
    average = lax.optimization_barrier(jnp.mean(floats, axis=-1, keepdims=True))
    centred = floats - average
    variance = lax.optimization_barrier(jnp.mean(centred * centred, axis=-1, keepdims=True))
    return (centred * lax.rsqrt(variance + EPSILON) * gain.astype(jnp.float32)).astype(jnp.bfloat16)

def attend(query_rows, key_rows, value_rows, alive_mask):
    count = query_rows.shape[0]
    block_rows = min(512, count)
    scaling = query_rows.shape[2] ** (-0.5)

    def one_head(operands):
        queries, keys_head, values_head = operands
        blocks = queries.reshape(count // block_rows, block_rows, queries.shape[1])

        def one_block(query_block):
            scores = jnp.dot(query_block, keys_head.T, preferred_element_type=jnp.float32) * scaling
            scores = jnp.where(alive_mask[None, :], scores, -1e+30)
            largest = lax.optimization_barrier(jnp.max(scores, axis=1, keepdims=True))
            exponent = jnp.exp(scores - largest)
            weights = (exponent / lax.optimization_barrier(jnp.sum(exponent, axis=1, keepdims=True))).astype(jnp.bfloat16)
            return jnp.dot(weights, values_head, preferred_element_type=jnp.float32).astype(jnp.bfloat16)
        return lax.map(one_block, blocks).reshape(count, queries.shape[1])
    heads_first = lax.map(one_head, (jnp.swapaxes(query_rows, 0, 1), jnp.swapaxes(key_rows, 0, 1), jnp.swapaxes(value_rows, 0, 1)))
    return jnp.swapaxes(heads_first, 0, 1).reshape(count, -1)

def encoder(embedded, alive_mask, gain_one, project_in, project_out, gain_two, up_weight, down_weight):
    count, width = embedded.shape
    normed = normalize(embedded, gain_one)
    projected = jnp.dot(normed, project_in, preferred_element_type=jnp.float32).astype(jnp.bfloat16)
    pieces = projected.reshape(count, 3, HEADS, width // HEADS)
    attended = attend(pieces[:, 0], pieces[:, 1], pieces[:, 2], alive_mask)
    mixed = (embedded.astype(jnp.float32) + jnp.dot(attended, project_out, preferred_element_type=jnp.float32)).astype(jnp.bfloat16)
    normed_two = normalize(mixed, gain_two)
    inner = jax.nn.gelu(jnp.dot(normed_two, up_weight, preferred_element_type=jnp.float32)).astype(jnp.bfloat16)
    return (mixed.astype(jnp.float32) + jnp.dot(inner, down_weight, preferred_element_type=jnp.float32)).astype(jnp.bfloat16)

def patch_conv(padded, first_kernel, frames):
    taps = jnp.stack([padded[:, offset:offset + STRIDE * (frames - 1) + 1:STRIDE] for offset in range(KERNEL)], axis=-1)
    summed = jnp.einsum('cfk,ko->fco', taps.astype(jnp.float32), first_kernel.astype(jnp.float32))
    return jax.nn.gelu(summed).astype(jnp.bfloat16)

def dilated(padded, weight, dilation, frames):
    summed = jnp.zeros((frames, padded.shape[1], weight.shape[2]), jnp.float32)
    for offset in range(3):
        window = padded[offset * dilation:offset * dilation + frames]
        summed = summed + jnp.einsum('fci,io->fco', window.astype(jnp.float32), weight[offset].astype(jnp.float32))
    return jax.nn.gelu(summed).astype(jnp.bfloat16)

def reference(samples, dead_channels, first_kernel, dilated_one, dilated_two, dilated_three, dilated_four, embed_weight, gain_one, project_in, project_out, gain_two, up_weight, down_weight):
    channel_ids = jnp.arange(NC, dtype=jnp.int32)
    alive_mask = jnp.logical_not(jnp.any(channel_ids[:, None] == dead_channels[None, :], axis=1))
    signal = jnp.where(alive_mask[:, None], samples, jnp.zeros_like(samples))
    rim_width = (KERNEL - STRIDE) // 2
    padded = jnp.pad(signal, ((0, 0), (rim_width, rim_width)))
    hidden = patch_conv(padded, first_kernel, F)
    for weight, dilation in zip((dilated_one, dilated_two, dilated_three, dilated_four), DILATIONS):
        extended = jnp.pad(hidden, ((dilation, dilation), (0, 0), (0, 0)))
        hidden = dilated(extended, weight, dilation, F)
    embedded = jnp.einsum('fci,io->fco', hidden.astype(jnp.float32), embed_weight.astype(jnp.float32)).astype(jnp.bfloat16)

    def per_frame(frame_tokens):
        return encoder(frame_tokens, alive_mask, gain_one, project_in, project_out, gain_two, up_weight, down_weight)
    return lax.map(per_frame, embedded)
```

```python
import functools

import jax
import jax.numpy as jnp
from jax import lax
from jax.experimental import pallas as pl
from jax.experimental.pallas import tpu as pltpu
from jax.sharding import PartitionSpec as P

HEADS = 8
STRIDE = 4
EPSILON = 1e-05
REACH = 15
CONV_ROWS = 384
QUERY_ROWS = 192
MESH = pl.DeviceIdType.MESH


def gelu(v):
    half = 0.5 * v
    return half + half * jnp.tanh(v * (0.7978845608028654 + 0.035677408136300125 * (v * v)))


def dot(a, b):
    return jnp.dot(a, b, preferred_element_type=jnp.float32)


def normalize(tokens, gain):
    floats = tokens.astype(jnp.float32)
    centred = floats - jnp.mean(floats, axis=-1, keepdims=True)
    variance = jnp.mean(centred * centred, axis=-1, keepdims=True)
    return (centred * lax.rsqrt(variance + EPSILON) * gain).astype(jnp.bfloat16)


def looped(count, body):
    if count == 1:
        body(0)
    else:
        lax.fori_loop(0, count, lambda i, c: (body(i), c)[1], 0)


def kernel(
    groups_t,
    groups_c,
    dead,
    samples,
    first_kernel,
    one,
    two_hbm,
    three_hbm,
    four_hbm,
    embed_hbm,
    gain_one,
    pin_hbm,
    pout_hbm,
    gain_two,
    up_hbm,
    down_hbm,
    out,
    gathered,
    signal,
    toeplitz,
    one_wide,
    h0,
    h1,
    h2,
    h3,
    embedded,
    qkv,
    attended,
    result,
    two,
    three,
    four,
    embed,
    pin,
    pout,
    up,
    down,
    weight_sem,
    send_sem,
    recv_sem,
    out_send,
    out_recv,
    own_sem,
):
    devices = groups_t * groups_c
    my_t, my_c = lax.axis_index("tm"), lax.axis_index("chan")
    me = my_t * groups_c + my_c
    held, slab = samples.shape
    pack_rows = gathered.shape[1]
    packs = held // pack_rows
    total_samples = groups_t * slab
    frames = total_samples // STRIDE
    tokens = groups_c * held
    frame = my_t * (slab // STRIDE) + my_c

    barrier = pltpu.get_barrier_semaphore()

    def greet(i):
        peer = lax.rem(me + 1 + i, devices)
        pl.semaphore_signal(
            barrier, inc=1, device_id=(peer // groups_c, lax.rem(peer, groups_c)), device_id_type=MESH
        )

    looped(devices - 1, greet)

    loads = [
        pltpu.make_async_copy(src, dst, weight_sem.at[i])
        for i, (src, dst) in enumerate(
            [
                (two_hbm, two),
                (three_hbm, three),
                (four_hbm, four),
                (embed_hbm, embed),
                (pin_hbm, pin),
                (pout_hbm, pout),
                (up_hbm, up),
                (down_hbm, down),
            ]
        )
    ]
    for load in loads:
        load.start()

    row_ids = lax.broadcasted_iota(jnp.int32, (held, slab), 0) + my_c * held
    dead_rows = row_ids < 0
    for i in range(dead.shape[0]):
        dead_rows = jnp.logical_or(dead_rows, row_ids == dead[i])
    own = jnp.where(dead_rows, 0.0, samples[...].astype(jnp.float32)).astype(jnp.bfloat16)
    for a in range(packs):
        gathered[me, :, a * slab : (a + 1) * slab] = own[a * pack_rows : (a + 1) * pack_rows, :]

    pl.semaphore_wait(barrier, devices - 1)

    def spread(peer):
        return pltpu.make_async_remote_copy(
            src_ref=gathered.at[me],
            dst_ref=gathered.at[me],
            send_sem=send_sem.at[peer],
            recv_sem=recv_sem.at[me],
            device_id=(peer // groups_c, lax.rem(peer, groups_c)),
            device_id_type=MESH,
        )

    looped(devices - 1, lambda i: spread(lax.rem(me + 1 + i, devices)).start())

    c1 = first_kernel.shape[1]
    width = (2 * REACH + 2) * c1
    pick = lax.broadcasted_iota(jnp.int32, (c1, width), 0) == lax.rem(
        lax.broadcasted_iota(jnp.int32, (c1, width), 1), c1
    )
    tiled = dot(first_kernel[...], pick.astype(jnp.float32).astype(jnp.bfloat16))
    for start in range(0, total_samples, 128):
        size = min(128, total_samples - start)
        at_sample = lax.broadcasted_iota(jnp.int32, (size, width), 0) + start
        at_frame = lax.broadcasted_iota(jnp.int32, (size, width), 1) // c1 + (frame - REACH)
        tap = at_sample - STRIDE * at_frame + (first_kernel.shape[0] - STRIDE) // 2
        tap = jnp.where(jnp.logical_and(at_frame >= 0, at_frame < frames), tap, -1)
        band = jnp.zeros((size, width), jnp.float32)
        for k in range(first_kernel.shape[0]):
            band = jnp.where(tap == k, tiled[k : k + 1, :], band)
        toeplitz[start : start + size, :] = band.astype(jnp.bfloat16)
    c2 = one.shape[1]
    one_wide[...] = jnp.zeros_like(one_wide)
    one_wide[: 3 * c1, :c2] = one[...]
    one_wide[2 * c1 : 5 * c1, c2:] = one[...]

    key_ids = lax.broadcasted_iota(jnp.int32, (1, tokens), 1)
    dead_keys = key_ids < 0
    for i in range(dead.shape[0]):
        dead_keys = jnp.logical_or(dead_keys, key_ids == dead[i])
    key_bias = jnp.where(dead_keys, -1e30, 0.0)

    def arrived(i):
        peer = lax.rem(me + 1 + i, devices)
        pltpu.make_async_remote_copy(
            src_ref=gathered.at[peer],
            dst_ref=gathered.at[peer],
            send_sem=send_sem.at[peer],
            recv_sem=recv_sem.at[peer],
            device_id=(peer // groups_c, lax.rem(peer, groups_c)),
            device_id_type=MESH,
        ).wait_recv()

    looped(devices - 1, arrived)

    for t in range(groups_t):
        for a in range(packs):
            signal[:, a * pack_rows : (a + 1) * pack_rows, t * slab : (t + 1) * slab] = gathered[
                t * groups_c : (t + 1) * groups_c, :, a * slab : (a + 1) * slab
            ]

    def inside(offset):
        at = frame + offset
        return jnp.logical_and(at >= 0, at < frames).astype(jnp.float32)

    for load in loads[:5]:
        load.wait()

    def convolve(block):
        chans = CONV_ROWS // held
        rows = pl.ds(pl.multiple_of(block * CONV_ROWS, CONV_ROWS), CONV_ROWS)
        waves = signal[pl.ds(block * chans, chans)].reshape(CONV_ROWS, total_samples)
        for q in range(width // 256):
            cols = slice(q * 256, (q + 1) * 256)
            h0[:, cols] = gelu(dot(waves, toeplitz[:, cols])).astype(jnp.bfloat16)
        later = lax.broadcasted_iota(jnp.int32, (1, 2 * c2), 1) >= c2
        for q in range(8):
            depth = min(5 * c1, width - 128 * q)
            summed = gelu(dot(h0[:, 128 * q : 128 * q + depth], one_wide[:depth, :]))
            keep = jnp.where(later, inside(4 * q + 2 - 14), inside(4 * q - 14))
            h1[:, 128 * q : 128 * (q + 1)] = (summed * keep).astype(jnp.bfloat16)
        for n in range(7):
            summed = gelu(dot(h1[:, 128 * n : 128 * n + 192], two[...]))
            h2[:, 128 * n : 128 * (n + 1)] = (summed * inside(4 * n - 12)).astype(jnp.bfloat16)
        for p in range(3):
            summed = gelu(dot(h2[:, 256 * p : 256 * p + 384], three[...]))
            h3[:, 256 * p : 256 * (p + 1)] = (summed * inside(8 * p - 8)).astype(jnp.bfloat16)
        features = gelu(dot(h3[...], four[...])).astype(jnp.bfloat16)
        embedded_rows = dot(features, embed[...]).astype(jnp.bfloat16)
        embedded[rows, :] = embedded_rows
        normed = normalize(embedded_rows, gain_one[...])
        for q in range(pin.shape[1] // 256):
            cols = slice(q * 256, (q + 1) * 256)
            qkv[rows, cols] = dot(normed, pin[:, cols]).astype(jnp.bfloat16)

    looped(tokens // CONV_ROWS, convolve)

    for load in loads[5:]:
        load.wait()

    model = embed.shape[1]
    head = model // HEADS
    blocks = tokens // QUERY_ROWS
    peers = QUERY_ROWS // held
    my_block = my_c // peers

    def back(peer):
        return pltpu.make_async_remote_copy(
            src_ref=result.at[peer],
            dst_ref=out.at[my_c],
            send_sem=out_send.at[peer],
            recv_sem=out_recv.at[my_c],
            device_id=(my_t, peer),
            device_id_type=MESH,
        )

    keep_own = pltpu.make_async_copy(result.at[my_c], out.at[my_c], own_sem)

    def encode(step):
        block = lax.rem(my_block + 1 + step, blocks)
        rows = pl.ds(pl.multiple_of(block * QUERY_ROWS, QUERY_ROWS), QUERY_ROWS)
        low = lax.broadcasted_iota(jnp.int32, (1, 2 * head), 1) < head
        for pair in range(HEADS // 2):
            base = pair * 2 * head
            queries = qkv[rows, base : base + 2 * head].astype(jnp.float32) * (head**-0.5)
            keys = qkv[:, model + base : model + base + 2 * head]
            values = qkv[:, 2 * model + base : 2 * model + base + 2 * head]
            parts = []
            for mask in (low, jnp.logical_not(low)):
                masked = jnp.where(mask, queries, 0.0).astype(jnp.bfloat16)
                scores = lax.dot_general(
                    masked, keys, (((1,), (1,)), ((), ())), preferred_element_type=jnp.float32
                )
                scores = scores + key_bias
                exponent = jnp.exp(scores - jnp.max(scores, axis=1, keepdims=True))
                total = jnp.sum(exponent, axis=1, keepdims=True)
                parts.append(dot(exponent.astype(jnp.bfloat16), values) / total)
            attended[:, base : base + 2 * head] = jnp.where(low, parts[0], parts[1]).astype(jnp.bfloat16)
        mixed = (embedded[rows, :].astype(jnp.float32) + dot(attended[...], pout[...])).astype(jnp.bfloat16)
        normed = normalize(mixed, gain_two[...])
        total = mixed.astype(jnp.float32)
        for q in range(up.shape[1] // 512):
            cols = slice(q * 512, (q + 1) * 512)
            inner = gelu(dot(normed, up[:, cols])).astype(jnp.bfloat16)
            total = total + dot(inner, down[cols, :])
        result[pl.ds(block * peers, peers)] = total.astype(jnp.bfloat16).reshape(peers, held, model)
        for i in range(peers):
            peer = block * peers + i

            @pl.when(peer != my_c)
            def _():
                back(peer).start()

            @pl.when(peer == my_c)
            def _():
                keep_own.start()

    looped(blocks, encode)

    looped(devices - 1, lambda i: spread(lax.rem(me + 1 + i, devices)).wait_send())

    def finish(i):
        peer = lax.rem(my_c + 1 + i, groups_c)
        back(peer).wait_send()
        pltpu.make_async_remote_copy(
            src_ref=result.at[peer],
            dst_ref=out.at[peer],
            send_sem=out_send.at[peer],
            recv_sem=out_recv.at[peer],
            device_id=(my_t, peer),
            device_id_type=MESH,
        ).wait_recv()

    looped(groups_c - 1, finish)
    keep_own.wait()


def per_device(
    samples,
    dead_channels,
    first_kernel,
    dilated_one,
    dilated_two,
    dilated_three,
    dilated_four,
    embed_weight,
    gain_one,
    project_in,
    project_out,
    gain_two,
    up_weight,
    down_weight,
):
    groups_t, groups_c = lax.axis_size("tm"), lax.axis_size("chan")
    held, slab = samples.shape
    assert slab // STRIDE == groups_c
    devices = groups_t * groups_c
    tokens = groups_c * held
    packs = 3 if slab * 3 <= 128 and held % 48 == 0 else 1
    model = embed_weight.shape[1]
    flat = [w.reshape(w.shape[0] * w.shape[1], w.shape[2]) for w in (dilated_one, dilated_two, dilated_three, dilated_four)]
    bf16 = jnp.bfloat16
    width = (2 * REACH + 2) * first_kernel.shape[1]
    vmem = pl.BlockSpec(memory_space=pltpu.VMEM)
    anywhere = pl.BlockSpec(memory_space=pl.ANY)
    like = lambda w: pltpu.VMEM(w.shape, w.dtype)
    return pl.pallas_call(
        functools.partial(kernel, groups_t, groups_c),
        out_shape=jax.ShapeDtypeStruct((groups_c, held, model), bf16),
        in_specs=[pl.BlockSpec(memory_space=pltpu.SMEM), vmem, vmem, vmem]
        + [anywhere] * 4
        + [vmem, anywhere, anywhere, vmem, anywhere, anywhere],
        out_specs=anywhere,
        scratch_shapes=[
            pltpu.VMEM((devices, held // packs, 128 if packs > 1 else slab), bf16),
            pltpu.VMEM((groups_c, held, groups_t * slab), bf16),
            pltpu.VMEM((groups_t * slab, width), bf16),
            pltpu.VMEM((5 * dilated_one.shape[1], 2 * dilated_one.shape[2]), bf16),
            pltpu.VMEM((CONV_ROWS, width), bf16),
            pltpu.VMEM((CONV_ROWS, 8 * 128), bf16),
            pltpu.VMEM((CONV_ROWS, 7 * 128), bf16),
            pltpu.VMEM((CONV_ROWS, 3 * 256), bf16),
            pltpu.VMEM((tokens, model), bf16),
            pltpu.VMEM((tokens, 3 * model), bf16),
            pltpu.VMEM((QUERY_ROWS, model), bf16),
            pltpu.VMEM((groups_c, held, model), bf16),
        ]
        + [like(w) for w in flat[1:]]
        + [like(w) for w in (embed_weight, project_in, project_out, up_weight, down_weight)]
        + [
            pltpu.SemaphoreType.DMA((8,)),
            pltpu.SemaphoreType.DMA((devices,)),
            pltpu.SemaphoreType.DMA((devices,)),
            pltpu.SemaphoreType.DMA((groups_c,)),
            pltpu.SemaphoreType.DMA((groups_c,)),
            pltpu.SemaphoreType.DMA,
        ],
        compiler_params=pltpu.CompilerParams(
            collective_id=0, has_side_effects=True, vmem_limit_bytes=56 * 2**20
        ),
    )(
        dead_channels,
        samples,
        first_kernel,
        *flat,
        embed_weight,
        gain_one.reshape(1, -1),
        project_in,
        project_out,
        gain_two.reshape(1, -1),
        up_weight,
        down_weight,
    )


def solution(mesh):
    return jax.shard_map(
        per_device,
        mesh=mesh,
        in_specs=(P("chan", "tm"), P(), P(), P(), P(), P(), P(), P(), P(), P(), P(), P(), P(), P()),
        out_specs=P("tm", "chan", None),
        check_vma=False,
    )
```

```python
import functools

import jax
import jax.numpy as jnp
from jax import lax
from jax.experimental import pallas as pl
from jax.experimental.pallas import tpu as pltpu
from jax.sharding import PartitionSpec as P

HEADS = 8
STRIDE = 4
EPSILON = 1e-05
REACH = 15
CONV_ROWS = 384
QUERY_ROWS = 192
STACK = 4
MESH = pl.DeviceIdType.MESH


def gelu(v):
    half = 0.5 * v
    return half + half * jnp.tanh(v * (0.7978845608028654 + 0.035677408136300125 * (v * v)))


def dot(a, b):
    return jnp.dot(a, b, preferred_element_type=jnp.float32)


def normalize(tokens, gain):
    floats = tokens.astype(jnp.float32)
    centred = floats - jnp.mean(floats, axis=-1, keepdims=True)
    variance = jnp.mean(centred * centred, axis=-1, keepdims=True)
    return (centred * lax.rsqrt(variance + EPSILON) * gain).astype(jnp.bfloat16)


def looped(count, body):
    if count == 1:
        body(0)
    else:
        lax.fori_loop(0, count, lambda i, c: (body(i), c)[1], 0)


def kernel(
    groups_t,
    groups_c,
    dead,
    samples,
    first_kernel,
    one,
    two_hbm,
    three_hbm,
    four_hbm,
    embed_hbm,
    gain_one,
    pin_hbm,
    pout_hbm,
    gain_two,
    up_hbm,
    down_hbm,
    out,
    gathered,
    signal,
    toeplitz,
    one_wide,
    h0,
    h1,
    h2,
    h3,
    embedded,
    qkv,
    attended,
    result,
    two,
    three,
    four,
    embed,
    pin,
    pout,
    up,
    down,
    weight_sem,
    send_sem,
    recv_sem,
    hand_send,
    hand_recv,
    out_send,
    out_recv,
    own_sem,
):
    my_t, my_c = lax.axis_index("tm"), lax.axis_index("chan")
    me = my_t * groups_c + my_c
    slab, held = samples.shape
    pack_rows = gathered.shape[1]
    packs = held // pack_rows
    total_samples = groups_t * slab
    frames = total_samples // STRIDE
    tokens = groups_c * held
    frame = my_t * (slab // STRIDE) + my_c

    barrier = pltpu.get_barrier_semaphore()

    def greet_chan(i):
        peer = lax.rem(my_c + 1 + i, groups_c)
        pl.semaphore_signal(barrier, inc=1, device_id=(my_t, peer), device_id_type=MESH)

    def greet_time(i):
        peer = lax.rem(my_t + 1 + i, groups_t)
        pl.semaphore_signal(barrier, inc=1, device_id=(peer, my_c), device_id_type=MESH)

    looped(groups_c - 1, greet_chan)
    looped(groups_t - 1, greet_time)

    loads = [
        pltpu.make_async_copy(src, dst, weight_sem.at[i])
        for i, (src, dst) in enumerate(
            [
                (two_hbm, two),
                (three_hbm, three),
                (four_hbm, four),
                (embed_hbm, embed),
                (pin_hbm, pin),
                (pout_hbm, pout),
                (up_hbm, up),
                (down_hbm, down),
            ]
        )
    ]
    for load in loads:
        load.start()

    row_ids = lax.broadcasted_iota(jnp.int32, (held, held), 0)
    alive = row_ids == lax.broadcasted_iota(jnp.int32, (held, held), 1)
    row_ids = row_ids + my_c * held
    for i in range(dead.shape[0]):
        alive = jnp.logical_and(alive, row_ids != dead[i])
    own = lax.dot_general(
        jnp.where(alive, 1.0, 0.0).astype(jnp.bfloat16),
        samples[...],
        (((1,), (1,)), ((), ())),
        preferred_element_type=jnp.float32,
    ).astype(jnp.bfloat16)
    for a in range(packs):
        gathered[me, :, a * slab : (a + 1) * slab] = own[a * pack_rows : (a + 1) * pack_rows, :]

    pl.semaphore_wait(barrier, groups_c + groups_t - 2)

    def spread(peer, slot):
        return pltpu.make_async_remote_copy(
            src_ref=gathered.at[my_t * groups_c + slot],
            dst_ref=gathered.at[my_t * groups_c + slot],
            send_sem=send_sem.at[peer],
            recv_sem=recv_sem.at[slot],
            device_id=(my_t, peer),
            device_id_type=MESH,
        )

    def hand(peer, slab_at):
        slots = pl.ds(slab_at * groups_c, groups_c)
        return pltpu.make_async_remote_copy(
            src_ref=gathered.at[slots],
            dst_ref=gathered.at[slots],
            send_sem=hand_send.at[peer],
            recv_sem=hand_recv.at[slab_at],
            device_id=(peer, my_c),
            device_id_type=MESH,
        )

    def chan_peer(i):
        return lax.rem(my_c + 1 + i, groups_c)

    def time_peer(i):
        return lax.rem(my_t + 1 + i, groups_t)

    looped(groups_c - 1, lambda i: spread(chan_peer(i), my_c).start())

    c1 = first_kernel.shape[1]
    width = (2 * REACH + 2) * c1
    pick = lax.broadcasted_iota(jnp.int32, (c1, width), 0) == lax.rem(
        lax.broadcasted_iota(jnp.int32, (c1, width), 1), c1
    )
    tiled = dot(first_kernel[...], pick.astype(jnp.float32).astype(jnp.bfloat16))
    c2 = one.shape[1]
    one_wide[...] = jnp.zeros_like(one_wide)
    one_wide[: 3 * c1, :c2] = one[...]
    one_wide[2 * c1 : 5 * c1, c2:] = one[...]

    key_ids = lax.broadcasted_iota(jnp.int32, (1, tokens), 1)
    dead_keys = key_ids < 0
    for i in range(dead.shape[0]):
        dead_keys = jnp.logical_or(dead_keys, key_ids == dead[i])
    key_bias = jnp.where(dead_keys, -1e30, 0.0)

    looped(groups_c - 1, lambda i: spread(chan_peer(i), chan_peer(i)).wait_recv())
    looped(groups_t - 1, lambda i: hand(time_peer(i), my_t).start())

    for start in range(0, total_samples, 128):
        size = min(128, total_samples - start)
        at_sample = lax.broadcasted_iota(jnp.int32, (size, width), 0) + start
        at_frame = lax.broadcasted_iota(jnp.int32, (size, width), 1) // c1 + (frame - REACH)
        tap = at_sample - STRIDE * at_frame + (first_kernel.shape[0] - STRIDE) // 2
        tap = jnp.where(jnp.logical_and(at_frame >= 0, at_frame < frames), tap, -1)
        band = jnp.zeros((size, width), jnp.float32)
        for k in range(first_kernel.shape[0]):
            band = jnp.where(tap == k, tiled[k : k + 1, :], band)
        toeplitz[start : start + size, :] = band.astype(jnp.bfloat16)

    looped(groups_t - 1, lambda i: hand(time_peer(i), time_peer(i)).wait_recv())

    for t in range(groups_t):
        for a in range(packs):
            signal[:, a * pack_rows : (a + 1) * pack_rows, t * slab : (t + 1) * slab] = gathered[
                t * groups_c : (t + 1) * groups_c, :, a * slab : (a + 1) * slab
            ]

    def inside(offset):
        at = frame + offset
        return jnp.logical_and(at >= 0, at < frames).astype(jnp.float32)

    for load in loads[:5]:
        load.wait()

    def convolve(block):
        chans = CONV_ROWS // held
        rows = pl.ds(pl.multiple_of(block * CONV_ROWS, CONV_ROWS), CONV_ROWS)
        waves = signal[pl.ds(block * chans, chans)].reshape(CONV_ROWS, total_samples)
        for q in range(width // 256):
            cols = slice(q * 256, (q + 1) * 256)
            h0[:, cols] = gelu(dot(waves, toeplitz[:, cols])).astype(jnp.bfloat16)
        later = lax.broadcasted_iota(jnp.int32, (1, 2 * c2), 1) >= c2
        for q in range(8):
            depth = min(5 * c1, width - 128 * q)
            summed = gelu(dot(h0[:, 128 * q : 128 * q + depth], one_wide[:depth, :]))
            keep = jnp.where(later, inside(4 * q + 2 - 14), inside(4 * q - 14))
            h1[:, 128 * q : 128 * (q + 1)] = (summed * keep).astype(jnp.bfloat16)
        for n in range(7):
            summed = gelu(dot(h1[:, 128 * n : 128 * n + 192], two[...]))
            h2[:, 128 * n : 128 * (n + 1)] = (summed * inside(4 * n - 12)).astype(jnp.bfloat16)
        for p in range(3):
            summed = gelu(dot(h2[:, 256 * p : 256 * p + 384], three[...]))
            h3[:, 256 * p : 256 * (p + 1)] = (summed * inside(8 * p - 8)).astype(jnp.bfloat16)
        features = gelu(dot(h3[...], four[...])).astype(jnp.bfloat16)
        embedded_rows = dot(features, embed[...]).astype(jnp.bfloat16)
        embedded[rows, :] = embedded_rows
        normed = normalize(embedded_rows, gain_one[...])
        for q in range(pin.shape[1] // 256):
            cols = slice(q * 256, (q + 1) * 256)
            qkv[rows, cols] = dot(normed, pin[:, cols]).astype(jnp.bfloat16)

    looped(tokens // CONV_ROWS, convolve)

    for load in loads[5:]:
        load.wait()

    model = embed.shape[1]
    head = model // HEADS
    blocks = tokens // QUERY_ROWS
    peers = QUERY_ROWS // held
    my_block = my_c // peers

    def back(peer):
        return pltpu.make_async_remote_copy(
            src_ref=result.at[peer],
            dst_ref=out.at[my_c],
            send_sem=out_send.at[peer],
            recv_sem=out_recv.at[my_c],
            device_id=(my_t, peer),
            device_id_type=MESH,
        )

    keep_own = pltpu.make_async_copy(result.at[my_c], out.at[my_c], own_sem)

    def encode(step):
        half = blocks // 2
        far = 1 - step // half
        side = lax.rem(my_block // half + far, 2)
        block = side * half + lax.rem(my_block + 1 + step, half)
        rows = pl.ds(pl.multiple_of(block * QUERY_ROWS, QUERY_ROWS), QUERY_ROWS)
        span = STACK * head
        lane_head = lax.broadcasted_iota(jnp.int32, (1, span), 1) // head
        for base in range(0, model, span):
            queries = qkv[rows, base : base + span].astype(jnp.float32) * (head**-0.5)
            keys = qkv[:, model + base : model + base + span]
            values = qkv[:, 2 * model + base : 2 * model + base + span]
            stacked = jnp.concatenate(
                [jnp.where(lane_head == h, queries, 0.0).astype(jnp.bfloat16) for h in range(STACK)], axis=0
            )
            scores = lax.dot_general(
                stacked, keys, (((1,), (1,)), ((), ())), preferred_element_type=jnp.float32
            )
            scores = scores + key_bias
            exponent = jnp.exp(scores - jnp.max(scores, axis=1, keepdims=True))
            total = jnp.sum(exponent, axis=1, keepdims=True)
            mean = dot(exponent.astype(jnp.bfloat16), values) / total
            merged = mean[:QUERY_ROWS]
            for h in range(1, STACK):
                merged = jnp.where(lane_head == h, mean[h * QUERY_ROWS : (h + 1) * QUERY_ROWS], merged)
            attended[:, base : base + span] = merged.astype(jnp.bfloat16)
        mixed = (embedded[rows, :].astype(jnp.float32) + dot(attended[...], pout[...])).astype(jnp.bfloat16)
        normed = normalize(mixed, gain_two[...])
        total = mixed.astype(jnp.float32)
        for q in range(up.shape[1] // 512):
            cols = slice(q * 512, (q + 1) * 512)
            inner = gelu(dot(normed, up[:, cols])).astype(jnp.bfloat16)
            total = total + dot(inner, down[cols, :])
        result[pl.ds(block * peers, peers)] = total.astype(jnp.bfloat16).reshape(peers, held, model)
        for i in range(peers):
            peer = block * peers + i

            @pl.when(peer != my_c)
            def _():
                back(peer).start()

            @pl.when(peer == my_c)
            def _():
                keep_own.start()

    looped(blocks, encode)

    looped(groups_c - 1, lambda i: spread(chan_peer(i), my_c).wait_send())
    looped(groups_t - 1, lambda i: hand(time_peer(i), my_t).wait_send())

    def finish(i):
        peer = lax.rem(my_c + 1 + i, groups_c)
        back(peer).wait_send()
        pltpu.make_async_remote_copy(
            src_ref=result.at[peer],
            dst_ref=out.at[peer],
            send_sem=out_send.at[peer],
            recv_sem=out_recv.at[peer],
            device_id=(my_t, peer),
            device_id_type=MESH,
        ).wait_recv()

    looped(groups_c - 1, finish)
    keep_own.wait()


def per_device(
    samples,
    dead_channels,
    first_kernel,
    dilated_one,
    dilated_two,
    dilated_three,
    dilated_four,
    embed_weight,
    gain_one,
    project_in,
    project_out,
    gain_two,
    up_weight,
    down_weight,
):
    groups_t, groups_c = lax.axis_size("tm"), lax.axis_size("chan")
    held, slab = samples.shape
    assert slab // STRIDE == groups_c
    devices = groups_t * groups_c
    tokens = groups_c * held
    packs = 3 if slab * 3 <= 128 and held % 48 == 0 else 1
    model = embed_weight.shape[1]
    flat = [w.reshape(w.shape[0] * w.shape[1], w.shape[2]) for w in (dilated_one, dilated_two, dilated_three, dilated_four)]
    bf16 = jnp.bfloat16
    width = (2 * REACH + 2) * first_kernel.shape[1]
    vmem = pl.BlockSpec(memory_space=pltpu.VMEM)
    anywhere = pl.BlockSpec(memory_space=pl.ANY)
    like = lambda w: pltpu.VMEM(w.shape, w.dtype)
    return pl.pallas_call(
        functools.partial(kernel, groups_t, groups_c),
        out_shape=jax.ShapeDtypeStruct((groups_c, held, model), bf16),
        in_specs=[pl.BlockSpec(memory_space=pltpu.SMEM), vmem, vmem, vmem]
        + [anywhere] * 4
        + [vmem, anywhere, anywhere, vmem, anywhere, anywhere],
        out_specs=anywhere,
        scratch_shapes=[
            pltpu.VMEM((devices, held // packs, 128 if packs > 1 else slab), bf16),
            pltpu.VMEM((groups_c, held, groups_t * slab), bf16),
            pltpu.VMEM((groups_t * slab, width), bf16),
            pltpu.VMEM((5 * dilated_one.shape[1], 2 * dilated_one.shape[2]), bf16),
            pltpu.VMEM((CONV_ROWS, width), bf16),
            pltpu.VMEM((CONV_ROWS, 8 * 128), bf16),
            pltpu.VMEM((CONV_ROWS, 7 * 128), bf16),
            pltpu.VMEM((CONV_ROWS, 3 * 256), bf16),
            pltpu.VMEM((tokens, model), bf16),
            pltpu.VMEM((tokens, 3 * model), bf16),
            pltpu.VMEM((QUERY_ROWS, model), bf16),
            pltpu.VMEM((groups_c, held, model), bf16),
        ]
        + [like(w) for w in flat[1:]]
        + [like(w) for w in (embed_weight, project_in, project_out, up_weight, down_weight)]
        + [
            pltpu.SemaphoreType.DMA((8,)),
            pltpu.SemaphoreType.DMA((groups_c,)),
            pltpu.SemaphoreType.DMA((groups_c,)),
            pltpu.SemaphoreType.DMA((groups_t,)),
            pltpu.SemaphoreType.DMA((groups_t,)),
            pltpu.SemaphoreType.DMA((groups_c,)),
            pltpu.SemaphoreType.DMA((groups_c,)),
            pltpu.SemaphoreType.DMA,
        ],
        compiler_params=pltpu.CompilerParams(
            collective_id=0, has_side_effects=True, vmem_limit_bytes=56 * 2**20
        ),
    )(
        dead_channels,
        samples.T,
        first_kernel,
        *flat,
        embed_weight,
        gain_one.reshape(1, -1),
        project_in,
        project_out,
        gain_two.reshape(1, -1),
        up_weight,
        down_weight,
    )


def solution(mesh):
    return jax.shard_map(
        per_device,
        mesh=mesh,
        in_specs=(P("chan", "tm"), P(), P(), P(), P(), P(), P(), P(), P(), P(), P(), P(), P(), P()),
        out_specs=P("tm", "chan", None),
        check_vma=False,
    )
```

```python
import functools

import jax
import jax.numpy as jnp
from jax import lax
from jax.experimental import pallas as pl
from jax.experimental.pallas import tpu as pltpu
from jax.sharding import PartitionSpec as P

HEADS = 8
STRIDE = 4
EPSILON = 1e-05
REACH = 15
CONV_ROWS = 384
QUERY_ROWS = 192
STACK = 4
MESH = pl.DeviceIdType.MESH


def gelu(v):
    half = 0.5 * v
    return half + half * jnp.tanh(v * (0.7978845608028654 + 0.035677408136300125 * (v * v)))


def dot(a, b):
    return jnp.dot(a, b, preferred_element_type=jnp.float32)


def normalize(tokens, gain):
    floats = tokens.astype(jnp.float32)
    centred = floats - jnp.mean(floats, axis=-1, keepdims=True)
    variance = jnp.mean(centred * centred, axis=-1, keepdims=True)
    return (centred * lax.rsqrt(variance + EPSILON) * gain).astype(jnp.bfloat16)


def third_offsets(gap):
    return sorted({part * gap + 8 * k for part in range(2) for k in (-1, 0, 1)})


def looped(count, body):
    if count == 1:
        body(0)
    else:
        lax.fori_loop(0, count, lambda i, c: (body(i), c)[1], 0)


def kernel(
    groups_t,
    groups_c,
    dead,
    samples,
    first_kernel,
    one,
    two_hbm,
    three_hbm,
    four_hbm,
    embed_hbm,
    gain_one,
    pin_hbm,
    pout_hbm,
    gain_two,
    up_hbm,
    down_hbm,
    out,
    gathered,
    signal,
    toeplitz,
    one_wide,
    h0,
    h1,
    h2,
    h3,
    embedded,
    normed_all,
    kv,
    attended,
    result,
    two,
    three,
    four,
    embed,
    pin,
    pout,
    up,
    down,
    weight_sem,
    send_sem,
    recv_sem,
    hand_send,
    hand_recv,
    out_send,
    out_recv,
    own_sem,
):
    my_t, my_c = lax.axis_index("tm"), lax.axis_index("chan")
    me = my_t * groups_c + my_c
    slab, held = samples.shape
    pack_rows = gathered.shape[1]
    packs = held // pack_rows
    total_samples = groups_t * slab
    frames = total_samples // STRIDE
    tokens = groups_c * held
    gap = groups_c // 2
    my_side, my_lane = my_c // gap, lax.rem(my_c, gap)
    frame = my_t * (slab // STRIDE) + my_lane

    barrier = pltpu.get_barrier_semaphore()

    def greet_chan(i):
        peer = lax.rem(my_c + 1 + i, groups_c)
        pl.semaphore_signal(barrier, inc=1, device_id=(my_t, peer), device_id_type=MESH)

    def greet_time(i):
        peer = lax.rem(my_t + 1 + i, groups_t)
        pl.semaphore_signal(barrier, inc=1, device_id=(peer, my_c), device_id_type=MESH)

    looped(groups_c - 1, greet_chan)
    looped(groups_t - 1, greet_time)

    loads = [
        pltpu.make_async_copy(src, dst, weight_sem.at[i])
        for i, (src, dst) in enumerate(
            [
                (two_hbm, two),
                (three_hbm, three),
                (four_hbm, four),
                (embed_hbm, embed),
                (pin_hbm, pin),
                (pout_hbm, pout),
                (up_hbm, up),
                (down_hbm, down),
            ]
        )
    ]
    for load in loads:
        load.start()

    row_ids = lax.broadcasted_iota(jnp.int32, (held, held), 0)
    alive = row_ids == lax.broadcasted_iota(jnp.int32, (held, held), 1)
    row_ids = row_ids + my_c * held
    for i in range(dead.shape[0]):
        alive = jnp.logical_and(alive, row_ids != dead[i])
    own = lax.dot_general(
        jnp.where(alive, 1.0, 0.0).astype(jnp.bfloat16),
        samples[...],
        (((1,), (1,)), ((), ())),
        preferred_element_type=jnp.float32,
    ).astype(jnp.bfloat16)
    for a in range(packs):
        gathered[me, :, a * slab : (a + 1) * slab] = own[a * pack_rows : (a + 1) * pack_rows, :]

    pl.semaphore_wait(barrier, groups_c + groups_t - 2)

    def spread(peer, slot):
        return pltpu.make_async_remote_copy(
            src_ref=gathered.at[my_t * groups_c + slot],
            dst_ref=gathered.at[my_t * groups_c + slot],
            send_sem=send_sem.at[peer],
            recv_sem=recv_sem.at[slot],
            device_id=(my_t, peer),
            device_id_type=MESH,
        )

    def hand(peer, slab_at):
        slots = pl.ds(slab_at * groups_c, groups_c)
        return pltpu.make_async_remote_copy(
            src_ref=gathered.at[slots],
            dst_ref=gathered.at[slots],
            send_sem=hand_send.at[peer],
            recv_sem=hand_recv.at[slab_at],
            device_id=(peer, my_c),
            device_id_type=MESH,
        )

    def chan_peer(i):
        return lax.rem(my_c + 1 + i, groups_c)

    def time_peer(i):
        return lax.rem(my_t + 1 + i, groups_t)

    looped(groups_c - 1, lambda i: spread(chan_peer(i), my_c).start())

    c1 = first_kernel.shape[1]
    width = toeplitz.shape[1]
    pick = lax.broadcasted_iota(jnp.int32, (c1, width), 0) == lax.rem(
        lax.broadcasted_iota(jnp.int32, (c1, width), 1), c1
    )
    tiled = dot(first_kernel[...], pick.astype(jnp.float32).astype(jnp.bfloat16))
    c2 = one.shape[1]
    one_wide[...] = jnp.zeros_like(one_wide)
    one_wide[: 3 * c1, :c2] = one[...]
    one_wide[2 * c1 : 5 * c1, c2:] = one[...]

    key_ids = lax.broadcasted_iota(jnp.int32, (1, tokens), 1)
    dead_keys = key_ids < 0
    for i in range(dead.shape[0]):
        dead_keys = jnp.logical_or(dead_keys, key_ids == dead[i])
    key_bias = jnp.where(dead_keys, -1e30, 0.0)

    looped(groups_c - 1, lambda i: spread(chan_peer(i), chan_peer(i)).wait_recv())
    looped(groups_t - 1, lambda i: hand(time_peer(i), my_t).start())

    for start in range(0, total_samples, 128):
        size = min(128, total_samples - start)
        at_sample = lax.broadcasted_iota(jnp.int32, (size, width), 0) + start
        at_frame = lax.broadcasted_iota(jnp.int32, (size, width), 1) // c1 + (frame - REACH)
        tap = at_sample - STRIDE * at_frame + (first_kernel.shape[0] - STRIDE) // 2
        tap = jnp.where(jnp.logical_and(at_frame >= 0, at_frame < frames), tap, -1)
        band = jnp.zeros((size, width), jnp.float32)
        for k in range(first_kernel.shape[0]):
            band = jnp.where(tap == k, tiled[k : k + 1, :], band)
        toeplitz[start : start + size, :] = band.astype(jnp.bfloat16)

    looped(groups_t - 1, lambda i: hand(time_peer(i), time_peer(i)).wait_recv())

    for t in range(groups_t):
        for a in range(packs):
            signal[:, a * pack_rows : (a + 1) * pack_rows, t * slab : (t + 1) * slab] = gathered[
                t * groups_c : (t + 1) * groups_c, :, a * slab : (a + 1) * slab
            ]

    def inside(offset):
        at = frame + offset
        return jnp.logical_and(at >= 0, at < frames).astype(jnp.float32)

    for load in loads[:5]:
        load.wait()

    model = embed.shape[1]
    head = model // HEADS

    def convolve(block):
        chans = CONV_ROWS // held
        rows = pl.ds(pl.multiple_of(block * CONV_ROWS, CONV_ROWS), CONV_ROWS)
        waves = signal[pl.ds(block * chans, chans)].reshape(CONV_ROWS, total_samples)
        for start in range(0, width, 256):
            cols = slice(start, min(start + 256, width))
            h0[:, cols] = gelu(dot(waves, toeplitz[:, cols])).astype(jnp.bfloat16)
        later = lax.broadcasted_iota(jnp.int32, (1, 2 * c2), 1) >= c2
        for q in range(h1.shape[1] // 128):
            depth = min(5 * c1, width - 128 * q)
            summed = gelu(dot(h0[:, 128 * q : 128 * q + depth], one_wide[:depth, :]))
            keep = jnp.where(later, inside(4 * q + 2 - 14), inside(4 * q - 14))
            h1[:, 128 * q : 128 * (q + 1)] = (summed * keep).astype(jnp.bfloat16)
        for n in range(h2.shape[1] // 128):
            summed = gelu(dot(h1[:, 128 * n : 128 * n + 192], two[...]))
            h2[:, 128 * n : 128 * (n + 1)] = (summed * inside(4 * n - 12)).astype(jnp.bfloat16)
        thirds = third_offsets(gap)
        for p, offset in enumerate(thirds):
            n = (offset + 8) // 4
            summed = gelu(dot(h2[:, 128 * n : 128 * n + 384], three[...]))
            h3[:, 256 * p : 256 * (p + 1)] = (summed * inside(offset)).astype(jnp.bfloat16)
        for part in range(2):
            summed = None
            for k in range(3):
                p = thirds.index(part * gap + 8 * (k - 1))
                term = dot(h3[:, 256 * p : 256 * (p + 1)], four[256 * k : 256 * (k + 1), :])
                summed = term if summed is None else summed + term
            embedded_rows = dot(gelu(summed).astype(jnp.bfloat16), embed[...]).astype(jnp.bfloat16)
            embedded[part, rows, :] = embedded_rows
            normed = normalize(embedded_rows, gain_one[...])
            normed_all[part, rows, :] = normed
            for q in range(kv.shape[2] // 256):
                cols = slice(q * 256, (q + 1) * 256)
                kv[part, rows, cols] = dot(
                    normed, pin[:, model + q * 256 : model + (q + 1) * 256]
                ).astype(jnp.bfloat16)

    looped(tokens // CONV_ROWS, convolve)

    for load in loads[5:]:
        load.wait()

    blocks = tokens // QUERY_ROWS
    peers = QUERY_ROWS // held

    def back(part, peer):
        return pltpu.make_async_remote_copy(
            src_ref=result.at[part * gap + peer],
            dst_ref=out.at[part * gap + my_lane],
            send_sem=out_send.at[part * gap + peer],
            recv_sem=out_recv.at[part * gap + my_lane],
            device_id=(my_t, my_side * gap + peer),
            device_id_type=MESH,
        )

    def keep_own(part):
        at = part * gap + my_lane
        return pltpu.make_async_copy(result.at[at], out.at[at], own_sem.at[part])

    def encode(step):
        part = step // (blocks // 2)
        block = lax.rem(step, blocks // 2)
        start = my_side * (tokens // 2) + block * QUERY_ROWS
        rows = pl.ds(pl.multiple_of(start, QUERY_ROWS), QUERY_ROWS)
        all_queries = dot(normed_all[part, rows, :], pin[:, :model]).astype(jnp.bfloat16)
        span = STACK * head
        lane_head = lax.broadcasted_iota(jnp.int32, (1, span), 1) // head
        for base in range(0, model, span):
            queries = all_queries[:, base : base + span].astype(jnp.float32) * (head**-0.5)
            keys = kv[part, :, base : base + span]
            values = kv[part, :, model + base : model + base + span]
            stacked = jnp.concatenate(
                [jnp.where(lane_head == h, queries, 0.0).astype(jnp.bfloat16) for h in range(STACK)], axis=0
            )
            scores = lax.dot_general(
                stacked, keys, (((1,), (1,)), ((), ())), preferred_element_type=jnp.float32
            )
            scores = scores + key_bias
            exponent = jnp.exp(scores - jnp.max(scores, axis=1, keepdims=True))
            total = jnp.sum(exponent, axis=1, keepdims=True)
            mean = dot(exponent.astype(jnp.bfloat16), values) / total
            merged = mean[:QUERY_ROWS]
            for h in range(1, STACK):
                merged = jnp.where(lane_head == h, mean[h * QUERY_ROWS : (h + 1) * QUERY_ROWS], merged)
            attended[:, base : base + span] = merged.astype(jnp.bfloat16)
        mixed = (embedded[part, rows, :].astype(jnp.float32) + dot(attended[...], pout[...])).astype(jnp.bfloat16)
        normed = normalize(mixed, gain_two[...])
        total = mixed.astype(jnp.float32)
        for q in range(up.shape[1] // 512):
            cols = slice(q * 512, (q + 1) * 512)
            inner = gelu(dot(normed, up[:, cols])).astype(jnp.bfloat16)
            total = total + dot(inner, down[cols, :])
        first = block * peers
        result[pl.ds(part * gap + first, peers)] = total.astype(jnp.bfloat16).reshape(peers, held, model)
        for i in range(peers):
            peer = first + i

            @pl.when(peer != my_lane)
            def _():
                back(part, peer).start()

            @pl.when(peer == my_lane)
            def _():
                keep_own(part).start()

    looped(blocks, encode)

    looped(groups_c - 1, lambda i: spread(chan_peer(i), my_c).wait_send())
    looped(groups_t - 1, lambda i: hand(time_peer(i), my_t).wait_send())

    def finish(i):
        peer = lax.rem(my_lane + 1 + i, gap)
        for part in range(2):
            back(part, peer).wait_send()
            pltpu.make_async_remote_copy(
                src_ref=result.at[part * gap + peer],
                dst_ref=out.at[part * gap + peer],
                send_sem=out_send.at[part * gap + peer],
                recv_sem=out_recv.at[part * gap + peer],
                device_id=(my_t, my_side * gap + peer),
                device_id_type=MESH,
            ).wait_recv()

    looped(gap - 1, finish)
    for part in range(2):
        keep_own(part).wait()


def per_device(
    samples,
    dead_channels,
    first_kernel,
    dilated_one,
    dilated_two,
    dilated_three,
    dilated_four,
    embed_weight,
    gain_one,
    project_in,
    project_out,
    gain_two,
    up_weight,
    down_weight,
):
    groups_t, groups_c = lax.axis_size("tm"), lax.axis_size("chan")
    held, slab = samples.shape
    assert slab // STRIDE == groups_c and groups_c % 8 == 0
    devices = groups_t * groups_c
    tokens = groups_c * held
    packs = 3 if slab * 3 <= 128 and held % 48 == 0 else 1
    model = embed_weight.shape[1]
    flat = [w.reshape(w.shape[0] * w.shape[1], w.shape[2]) for w in (dilated_one, dilated_two, dilated_three, dilated_four)]
    bf16 = jnp.bfloat16
    gap = groups_c // 2
    width = (2 * REACH + gap + 2) * first_kernel.shape[1]
    vmem = pl.BlockSpec(memory_space=pltpu.VMEM)
    anywhere = pl.BlockSpec(memory_space=pl.ANY)
    like = lambda w: pltpu.VMEM(w.shape, w.dtype)
    return pl.pallas_call(
        functools.partial(kernel, groups_t, groups_c),
        out_shape=jax.ShapeDtypeStruct((groups_c, held, model), bf16),
        in_specs=[pl.BlockSpec(memory_space=pltpu.SMEM), vmem, vmem, vmem]
        + [anywhere] * 4
        + [vmem, anywhere, anywhere, vmem, anywhere, anywhere],
        out_specs=anywhere,
        scratch_shapes=[
            pltpu.VMEM((devices, held // packs, 128 if packs > 1 else slab), bf16),
            pltpu.VMEM((groups_c, held, groups_t * slab), bf16),
            pltpu.VMEM((groups_t * slab, width), bf16),
            pltpu.VMEM((5 * dilated_one.shape[1], 2 * dilated_one.shape[2]), bf16),
            pltpu.VMEM((CONV_ROWS, width), bf16),
            pltpu.VMEM((CONV_ROWS, ((28 + gap) // 2 + 2) // 2 * 128), bf16),
            pltpu.VMEM((CONV_ROWS, ((24 + gap) // 4 + 1) * 128), bf16),
            pltpu.VMEM((CONV_ROWS, len(third_offsets(gap)) * 256), bf16),
            pltpu.VMEM((2, tokens, model), bf16),
            pltpu.VMEM((2, tokens, model), bf16),
            pltpu.VMEM((2, tokens, 2 * model), bf16),
            pltpu.VMEM((QUERY_ROWS, model), bf16),
            pltpu.VMEM((groups_c, held, model), bf16),
        ]
        + [like(w) for w in flat[1:]]
        + [like(w) for w in (embed_weight, project_in, project_out, up_weight, down_weight)]
        + [
            pltpu.SemaphoreType.DMA((8,)),
            pltpu.SemaphoreType.DMA((groups_c,)),
            pltpu.SemaphoreType.DMA((groups_c,)),
            pltpu.SemaphoreType.DMA((groups_t,)),
            pltpu.SemaphoreType.DMA((groups_t,)),
            pltpu.SemaphoreType.DMA((groups_c,)),
            pltpu.SemaphoreType.DMA((groups_c,)),
            pltpu.SemaphoreType.DMA((2,)),
        ],
        compiler_params=pltpu.CompilerParams(
            collective_id=0, has_side_effects=True, vmem_limit_bytes=56 * 2**20
        ),
    )(
        dead_channels,
        samples.T,
        first_kernel,
        *flat,
        embed_weight,
        gain_one.reshape(1, -1),
        project_in,
        project_out,
        gain_two.reshape(1, -1),
        up_weight,
        down_weight,
    )


def solution(mesh):
    return jax.shard_map(
        per_device,
        mesh=mesh,
        in_specs=(P("chan", "tm"), P(), P(), P(), P(), P(), P(), P(), P(), P(), P(), P(), P(), P()),
        out_specs=P("tm", "chan", None),
        check_vma=False,
    )
```
